32 devices in a mesh: groups: 2 (over y), gx: 4 (over z), gy: 2 (over core), gz: 2 (over x).
Axes of the slice: x: 2, y: 2, z: 4, core: 2. Of those that a mesh axis runs over, the one named last changes fastest.
Arguments:
- tokens: bfloat16 [6144, 4096], P(('groups', 'gx', 'gz'), 'gy'), parts along dimension 0, may hold values from -6 to 6
- weights: bfloat16 [4096, 14336], P('gy', ('gz', 'gx')), may hold values from -0.09375 to 0.09375
- counts: int32 [8], P(('groups', 'gx')), parts along dimension 0, may hold values from 1 to 6
Outputs:
- projected: bfloat16 [6144, 14336], P(('groups', 'gx', 'gy'), 'gz'), parts along dimension 0
The draws below stay inside these ranges and needn't reach their ends.
There are 2 independent parts, one for each index of `groups`. The reference program is written for one: setup_inputs(seed, part) draws one part's arguments, and reference() takes and returns one part's arrays. A program takes and returns all parts, laid end to end along the dimension named above; an argument that names none is the same for every part. Nothing has to cross between parts.
Inputs may be any that keep to these rules, and one draw needn't show every extreme that they name: counts[s] is the number of whole blocks of 128 rows, at the start of token shard s, that hold valid rows.
All inputs are finite; a program needn't handle non-finite values.
Results may differ from the reference program's by a relative error of at most 0.001.
Values may be sent and summed in bfloat16 or wider, within the bound.
A program may use at most 128 MiB of HBM per device.

```python
import jax
import jax.numpy as jnp
from jax import lax

D = 4096
FF = 14336
BLOCK = 128
BLOCKS_X = 6
TOK_X = 768
ROWS = 3072
N_GX = 4


def set_ends(values, own_key, low, high):
    index_at = [jax.random.randint(jax.random.fold_in(own_key, axis), (), 0, length) for axis, length in enumerate(values.shape)]
    main_axis = values.shape.index(max(values.shape))
    beside = index_at[:main_axis] + [(index_at[main_axis] + 1) % values.shape[main_axis]] + index_at[main_axis + 1:]
    return values.at[tuple(index_at)].set(low).at[tuple(beside)].set(high)


def block_levels(rng, extent, cuts, smallest, top_value):
    factor_of, own = 1.0, jax.random.fold_in(rng, 6)
    for dim, blocks in cuts:
        heights = jnp.exp(jax.random.uniform(jax.random.fold_in(own, dim), (blocks,), jnp.float32, smallest / len(cuts), top_value / len(cuts)))
        factor_of = factor_of * jnp.repeat(heights, extent[dim] // blocks).reshape([-1 if axis == dim else 1 for axis in range(len(extent))])
    return factor_of


def noise(own_key, extent, width, reach, cuts=(), kind=jnp.bfloat16):
    factor_of = block_levels(own_key, extent, cuts, -0.22, 0.18) if cuts else 1.0
    array = jax.random.normal(own_key, extent, jnp.float32) * width * factor_of
    return jnp.minimum(jnp.maximum(array, -reach), reach).astype(kind)


def setup_inputs(seed: int = 0, part: int = 0) -> dict:
    arg_keys = jax.random.split(jax.random.key(seed), 4)
    own_keys = jax.random.split(jax.random.fold_in(arg_keys[3], part), 4)
    tokens = noise(own_keys[0], (ROWS, D), 1.0, 6.0, ((0, 8), (1, 2)))
    weights = noise(arg_keys[1], (D, FF), D ** -0.5, 0.09375, ((0, 2), (1, 8)))
    counts = set_ends(jax.random.randint(own_keys[2], (N_GX,), 1, BLOCKS_X + 1), jax.random.fold_in(own_keys[2], 1), 1, BLOCKS_X).astype(jnp.int32)
    return {"tokens": tokens, "weights": weights, "counts": counts}


def reference(tokens, weights, counts):
    shards = tokens.reshape(N_GX, TOK_X, D)
    row_index = jnp.arange(TOK_X, dtype=jnp.int32)

    def one_shard(packed):
        shard_rows, shard_count = packed
        product = jnp.dot(shard_rows, weights, preferred_element_type=jnp.float32)
        valid = row_index < shard_count * BLOCK
        return jnp.where(valid[:, None], product, jnp.float32(0.0)).astype(jnp.bfloat16)

    result = lax.map(one_shard, (shards, counts.astype(jnp.int32)))
    return result.reshape(ROWS, FF)
```

```python
import functools

import jax
import jax.numpy as jnp
from jax import lax
from jax.experimental import pallas as pl
from jax.experimental.pallas import tpu as pltpu
from jax.sharding import PartitionSpec as P

BLOCK = 128
MESH = pl.DeviceIdType.MESH


def block_product(left_rows, column_piece, valid_count):
    total_rows = left_rows.shape[0]
    row_index = jnp.arange(total_rows, dtype=jnp.int32)
    product = jnp.dot(left_rows, column_piece, preferred_element_type=jnp.float32)
    return jnp.where((row_index < valid_count * BLOCK)[:, None], product, jnp.float32(0.0))


def shards_general(tokens, weights, counts):
    valid_count = counts[0]
    shard_rows = lax.all_gather(tokens, "gz", axis=0, tiled=True)
    partial_value = block_product(
        shard_rows, lax.all_gather(weights, "gx", axis=1, tiled=True), valid_count
    )
    result = lax.psum_scatter(partial_value, "gy", scatter_dimension=0, tiled=True)
    return result.astype(jnp.bfloat16)


def kernel(n, nb, tile, tokens, weights, out, t, w, o,
           load_sem, init_send, init_recv, w_load, w_send, w_recv,
           up_send, down_send, x_send, t_recv, o_send, o_recv, o_copy):
    z, g, x = lax.axis_index("gx"), lax.axis_index("gy"), lax.axis_index("gz")
    depth, cols = weights.shape
    line = g == x

    barrier = pltpu.get_barrier_semaphore()
    for d in range(1, n):
        pl.semaphore_signal(barrier, inc=1, device_id={"gx": lax.rem(z + d, n)}, device_id_type=MESH)
    pl.semaphore_signal(barrier, inc=1, device_id={"gy": 1 - g}, device_id_type=MESH)
    pl.semaphore_signal(barrier, inc=1, device_id={"gz": 1 - x}, device_id_type=MESH)
    pl.semaphore_wait(barrier, n + 1)

    my_depth = pl.ds(pl.multiple_of(g * depth, depth), depth)

    def rows(j):
        return pl.ds(pl.multiple_of(j * BLOCK, BLOCK), BLOCK)

    def load(j):
        return pltpu.make_async_copy(tokens.at[rows(j)], t.at[z, j, :, my_depth], load_sem.at[j])

    def hand(j):
        return pltpu.make_async_remote_copy(
            tokens.at[rows(j)], t.at[z, j, :, my_depth], init_send.at[j], init_recv.at[j],
            device_id={"gy": 1 - g}, device_id_type=MESH)

    def relay(s, j, sem, where):
        return pltpu.make_async_remote_copy(
            t.at[s, j], t.at[s, j], sem.at[s, j], t_recv.at[s, j],
            device_id=where, device_id_type=MESH)

    def up(s, j):
        return relay(s, j, up_send, {"gx": jnp.minimum(z + 1, n - 1)})

    def down(s, j):
        return relay(s, j, down_send, {"gx": jnp.maximum(z - 1, 0)})

    def across(s, j):
        return relay(s, j, x_send, {"gz": 1 - x})

    def columns(c):
        return pl.ds(pl.multiple_of(c * cols, cols), cols)

    def give(s, j):
        return pltpu.make_async_remote_copy(
            o.at[s, j], out.at[rows(j), columns(z)], o_send.at[s, j], o_recv.at[z, j],
            device_id={"gx": s}, device_id_type=MESH)

    def take(c, j):
        return pltpu.make_async_remote_copy(
            o.at[c, j], out.at[rows(j), columns(c)], o_send.at[c, j], o_recv.at[c, j],
            device_id={"gx": c}, device_id_type=MESH)

    def keep(j):
        return pltpu.make_async_copy(o.at[z, j], out.at[rows(j), columns(z)], o_copy.at[j])

    w_mine = pltpu.make_async_copy(weights, w.at[my_depth], w_load)
    w_other = pltpu.make_async_remote_copy(
        weights, w.at[my_depth], w_send, w_recv, device_id={"gy": 1 - g}, device_id_type=MESH)

    @pl.when(line)
    def _():
        for j in range(nb):
            load(j).start()
    @pl.when(jnp.logical_not(line))
    def _():
        for j in range(nb):
            hand(j).start()
    w_mine.start()
    w_other.start()

    @pl.when(line)
    def _():
        for j in range(nb):
            load(j).wait()
            hand(j).wait_recv()
            @pl.when(z < n - 1)
            def _():
                up(z, j).start()
            @pl.when(z > 0)
            def _():
                down(z, j).start()
            across(z, j).start()

    def multiply(s, j):
        @pl.loop(0, cols // tile)
        def _(i):
            at = pl.ds(pl.multiple_of(i * tile, tile), tile)
            o[s, j, :, at] = jnp.dot(
                t[s, j], w[:, at], preferred_element_type=jnp.float32).astype(o.dtype)

    w_mine.wait()
    w_other.wait()

    per = 2 * nb

    @pl.loop(0, (n - 1) * per)
    def _(i):
        d, r = i // per + 1, i % per
        j = r // 2
        s = z + d * (1 - 2 * (r % 2))

        @pl.when((s >= 0) & (s < n))
        def _():
            across(s, j).wait_recv()

            @pl.when(line)
            def _():
                @pl.when((s < z) & (z < n - 1))
                def _():
                    up(s, j).start()
                @pl.when((s > z) & (z > 0))
                def _():
                    down(s, j).start()
                across(s, j).start()
            multiply(s, j)
            give(s, j).start()

    @pl.when(jnp.logical_not(line))
    def _():
        for j in range(nb):
            across(z, j).wait_recv()

    @pl.loop(0, nb)
    def _(j):
        multiply(z, j)
        keep(j).start()

    @pl.when(jnp.logical_not(line))
    def _():
        for j in range(nb):
            hand(j).wait_send()

    @pl.loop(0, n * nb)
    def _(i):
        s, j = i // nb, i % nb

        @pl.when(line)
        def _():
            @pl.when((s <= z) & (z < n - 1))
            def _():
                up(s, j).wait_send()
            @pl.when((s >= z) & (z > 0))
            def _():
                down(s, j).wait_send()
            across(s, j).wait_send()

        @pl.when(s != z)
        def _():
            give(s, j).wait_send()
            take(s, j).wait_recv()

    for j in range(nb):
        keep(j).wait()


def shards_kernel(n, tokens, weights, counts):
    rows, depth = tokens.shape
    cols = weights.shape[1]
    nb = rows // BLOCK
    dma = pltpu.SemaphoreType.DMA
    product = pl.pallas_call(
        functools.partial(kernel, n, nb, 256),
        out_shape=jax.ShapeDtypeStruct((rows, n * cols), jnp.bfloat16),
        in_specs=[pl.BlockSpec(memory_space=pl.ANY)] * 2,
        out_specs=pl.BlockSpec(memory_space=pl.ANY),
        scratch_shapes=[
            pltpu.VMEM((n, nb, BLOCK, 2 * depth), jnp.bfloat16),
            pltpu.VMEM((2 * depth, cols), jnp.bfloat16),
            pltpu.VMEM((n, nb, BLOCK, cols), jnp.bfloat16),
            dma((nb,)), dma((nb,)), dma((nb,)),
            dma, dma, dma,
            dma((n, nb)), dma((n, nb)), dma((n, nb)), dma((n, nb)),
            dma((n, nb)), dma((n, nb)), dma((nb,)),
        ],
        compiler_params=pltpu.CompilerParams(
            collective_id=0, has_side_effects=True, vmem_limit_bytes=50 * 2**20),
    )(tokens, weights)
    row_index = lax.axis_index("gy") * rows + jnp.arange(rows, dtype=jnp.int32)
    return jnp.where((row_index < counts[0] * BLOCK)[:, None], product, jnp.bfloat16(0.0))


def shards(sizes, tokens, weights, counts):
    rows, depth = tokens.shape
    cols = weights.shape[1]
    n = sizes["gx"]
    held = 2 * (2 * n * rows * depth + 2 * depth * cols + n * rows * cols)
    if (sizes["gz"] == 2 and sizes["gy"] == 2 and rows % BLOCK == 0 and cols % 256 == 0
            and depth % 128 == 0 and held < 45 * 2**20):
        return shards_kernel(n, tokens, weights, counts)
    return shards_general(tokens, weights, counts)


def solution(mesh):
    return jax.shard_map(
        functools.partial(shards, dict(mesh.shape)),
        mesh=mesh,
        in_specs=(P(("groups", "gx", "gz"), "gy"), P("gy", ("gz", "gx")), P(("groups", "gx"))),
        out_specs=P(("groups", "gx", "gy"), "gz"),
        check_vma=False,
    )
```

```python
import functools

import jax
import jax.numpy as jnp
from jax import lax
from jax.experimental import pallas as pl
from jax.experimental.pallas import tpu as pltpu
from jax.sharding import PartitionSpec as P

BLOCK = 128
LANES = 128
MESH = pl.DeviceIdType.MESH


def block_product(left_rows, column_piece, valid_count):
    total_rows = left_rows.shape[0]
    row_index = jnp.arange(total_rows, dtype=jnp.int32)
    product = jnp.dot(left_rows, column_piece, preferred_element_type=jnp.float32)
    return jnp.where((row_index < valid_count * BLOCK)[:, None], product, jnp.float32(0.0))


def shards_general(tokens, weights, counts):
    valid_count = counts[0]
    shard_rows = lax.all_gather(tokens, "gz", axis=0, tiled=True)
    partial_value = block_product(
        shard_rows, lax.all_gather(weights, "gx", axis=1, tiled=True), valid_count
    )
    result = lax.psum_scatter(partial_value, "gy", scatter_dimension=0, tiled=True)
    return result.astype(jnp.bfloat16)


def kernel(tokens, weights, out, t, wo, wr, oo, op,
           load_sem, tx_send, tz_send, td_send, chip_send, t_recv,
           wo_load, wo_send, wo_recv, wr_send, wr_recv, y_send, y_recv,
           oo_send, op_send, o_recv):
    y, z = lax.axis_index("groups"), lax.axis_index("gx")
    g, x = lax.axis_index("gy"), lax.axis_index("gz")
    rows, depth = tokens.shape
    half = weights.shape[1] // 2
    chunks = half // LANES
    side = z // 2
    role = (z + side) % 2
    mate = 4 * side + 1 - z
    far = 2 - side
    hub = role == 1
    line = g == y

    barrier = pltpu.get_barrier_semaphore()
    for d in range(4):
        for e in range(2):
            if d or e:
                pl.semaphore_signal(barrier, inc=1, device_id={"gx": (z + d) % 4, "gy": (g + e) % 2},
                                    device_id_type=MESH)
    pl.semaphore_signal(barrier, inc=1, device_id={"gz": 1 - x}, device_id_type=MESH)
    pl.semaphore_signal(barrier, inc=1, device_id={"groups": 1 - y}, device_id_type=MESH)
    pl.semaphore_wait(barrier, 9)

    def remote(src, dst, send, recv, **where):
        return pltpu.make_async_remote_copy(src, dst, send, recv, device_id=where, device_id_type=MESH)

    def cut(k):
        return pl.ds(pl.multiple_of(k * depth, depth), depth)

    def slot(r, h, k):
        return t.at[r, h, :, cut(k)]

    own = slot(role, x, g)
    load = pltpu.make_async_copy(tokens, own, load_sem)
    to_x = remote(tokens, own, tx_send, t_recv.at[role, x, g], gz=1 - x)
    to_z = remote(tokens, own, tz_send, t_recv.at[role, x, g], gx=mate)
    relay_x = remote(slot(1 - role, x, g), slot(1 - role, x, g), td_send,
                     t_recv.at[1 - role, x, g], gz=1 - x)

    def to_chip(r, h, k):
        src = tokens if r is role and h is x else slot(r, h, k)
        return remote(src, slot(r, h, k), chip_send.at[r, h], t_recv.at[r, h, k], gy=1 - g)

    def arrived(r, h, k):
        return remote(slot(r, h, k), slot(r, h, k), td_send, t_recv.at[r, h, k], gy=1 - g)

    def part(p):
        return pl.ds(pl.multiple_of(p * half, LANES), half)

    wo_mine = pltpu.make_async_copy(weights.at[:, part(g)], wo.at[cut(g)], wo_load)
    wo_other = remote(weights.at[:, part(1 - g)], wo.at[cut(g)], wo_send, wo_recv, gy=1 - g)

    def lanes(ab):
        return pl.ds(pl.multiple_of(ab * LANES, LANES), LANES)

    def push(i):
        src = weights.at[:, pl.ds(pl.multiple_of(y * half + i * LANES, LANES), LANES)]
        return remote(src, wr.at[i, cut(g), lanes(1 - role)], wr_send.at[i],
                      wr_recv.at[1 - role, i, g], gx=far, gy=y)

    def pushed(ab, i, k):
        dst = wr.at[i, cut(k), lanes(ab)]
        return remote(dst, dst, wr_send.at[i], wr_recv.at[ab, i, k], gy=1 - g)

    def pass_on(ab, i):
        dst = wr.at[i, :, lanes(ab)]
        return remote(dst, dst, y_send.at[ab, i], y_recv.at[ab, i], groups=1 - y)

    def layer(r):
        return (1 - r) * 3 * side + r * (1 + side)

    def own_dst(c, p):
        return out.at[:, pl.ds(pl.multiple_of(c * 2 * half + p * half, LANES), half)]

    def far_layer(ab):
        return (1 - ab) * far + ab * 3 * (1 - side)

    def far_dst(ab, p, i):
        return out.at[:, pl.ds(
            pl.multiple_of(far_layer(ab) * 2 * half + p * half + i * LANES, LANES), LANES)]

    def send_own(r, h):
        return remote(oo.at[r, h], own_dst(z, g), oo_send.at[r, h], o_recv.at[role, g, 0],
                      gx=layer(r), gy=h)

    def keep_own():
        return pltpu.make_async_copy(oo.at[role, g], own_dst(z, g), oo_send.at[role, g])

    def send_far(ab, i, r, h):
        return remote(op.at[i, r, h, :, lanes(ab)], far_dst(ab, g, i), op_send.at[ab, i, r, h],
                      o_recv.at[2 + ab, g, i], gx=layer(r), gy=h)

    def keep_far(ab, i):
        return pltpu.make_async_copy(op.at[i, role, g, :, lanes(ab)], far_dst(ab, g, i),
                                     op_send.at[ab, i, role, g])

    to_x.start()
    to_z.start()
    load.start()
    to_chip(role, x, g).start()

    @pl.loop(0, chunks)
    def _(i):
        push(i).start()
    wo_other.start()
    wo_mine.start()

    def pass_step(ab, i):
        @pl.when(hub & line)
        def _():
            pushed(ab, i, 0).wait_recv()
            pushed(ab, i, 1).wait_recv()
            pass_on(ab, i).start()

    def own_half(r):
        @pl.loop(0, 2)
        def _(h):
            @pl.loop(0, half // 256)
            def _(q):
                at = pl.ds(pl.multiple_of(q * 256, 256), 256)
                oo[r, h, :, at] = jnp.dot(
                    t[r, h], wo[:, at], preferred_element_type=jnp.float32).astype(oo.dtype)
            if half % 256:
                at = pl.ds(half // 256 * 256, half % 256)
                oo[r, h, :, at] = jnp.dot(
                    t[r, h], wo[:, at], preferred_element_type=jnp.float32).astype(oo.dtype)
            mine = (r == role) & (h == g)

            @pl.when(mine)
            def _():
                keep_own().start()

            @pl.when(jnp.logical_not(mine))
            def _():
                send_own(r, h).start()

    def far_pair(i):
        @pl.when(hub)
        def _():
            @pl.when(jnp.logical_not(line))
            def _():
                pass_on(0, i).wait_recv()
                pass_on(1, i).wait_recv()

            @pl.loop(0, 4)
            def _(b):
                r, h = b // 2, b % 2
                op[i, r, h] = jnp.dot(
                    t[r, h], wr[i], preferred_element_type=jnp.float32).astype(op.dtype)
                mine = (r == role) & (h == g)

                @pl.when(mine)
                def _():
                    keep_far(0, i).start()
                    keep_far(1, i).start()

                @pl.when(jnp.logical_not(mine))
                def _():
                    send_far(0, i, r, h).start()
                    send_far(1, i, r, h).start()

    lead = min(3, chunks)
    order = [(0, i) for i in range(lead)]
    for i in range(chunks):
        order.append((1, i))
        if i + lead < chunks:
            order.append((0, i + lead))
    order = order[::-1]

    def next_pass():
        if order:
            pass_step(*order.pop())

    next_pass()
    next_pass()
    arrived(role, 1 - x, g).wait_recv()
    to_chip(role, 1 - x, g).start()
    arrived(1 - role, x, g).wait_recv()
    relay_x.start()
    to_chip(1 - role, x, g).start()
    next_pass()
    load.wait()
    arrived(role, x, 1 - g).wait_recv()
    arrived(role, 1 - x, 1 - g).wait_recv()
    wo_mine.wait()
    wo_other.wait()
    next_pass()
    own_half(role)
    next_pass()
    arrived(1 - role, 1 - x, g).wait_recv()
    to_chip(1 - role, 1 - x, g).start()
    next_pass()
    arrived(1 - role, x, 1 - g).wait_recv()
    arrived(1 - role, 1 - x, 1 - g).wait_recv()
    own_half(1 - role)
    done = 0
    while done < chunks:
        next_pass()
        if (1, done) not in order and (0, done) not in order:
            far_pair(done)
            done += 1

    to_x.wait_send()
    to_z.wait_send()
    relay_x.wait_send()
    for b in range(4):
        to_chip(b // 2, b % 2, g).wait_send()

    @pl.loop(0, 4)
    def _(b):
        r, h = b // 2, b % 2
        mine = (r == role) & (h == g)

        @pl.when(mine)
        def _():
            keep_own().wait()

        @pl.when(jnp.logical_not(mine))
        def _():
            send_own(r, h).wait_send()

        @pl.when(jnp.logical_not(mine))
        def _():
            remote(oo.at[0, 0], own_dst(layer(r), h), oo_send.at[0, 0], o_recv.at[r, h, 0],
                   gy=1 - g).wait_recv()

    @pl.loop(0, chunks)
    def _(i):
        push(i).wait_send()

        @pl.loop(0, 2)
        def _(ab):
            @pl.when(hub & line)
            def _():
                pass_on(ab, i).wait_send()

            @pl.when(hub)
            def _():
                keep_far(ab, i).wait()

                @pl.loop(0, 4)
                def _(b):
                    r, h = b // 2, b % 2

                    @pl.when(jnp.logical_not((r == role) & (h == g)))
                    def _():
                        send_far(ab, i, r, h).wait_send()

            @pl.loop(0, 2)
            def _(p):
                @pl.when(jnp.logical_not(hub & (p == g)))
                def _():
                    remote(op.at[0, 0, 0, :, lanes(0)], far_dst(ab, p, i), op_send.at[0, 0, 0, 0],
                           o_recv.at[2 + ab, p, i], gy=1 - g).wait_recv()


def shards_kernel(tokens, weights, counts):
    rows, depth = tokens.shape
    cols = weights.shape[1]
    half = cols // 2
    chunks = half // LANES
    dma = pltpu.SemaphoreType.DMA
    product = pl.pallas_call(
        kernel,
        out_shape=jax.ShapeDtypeStruct((rows, 4 * cols), jnp.bfloat16),
        in_specs=[pl.BlockSpec(memory_space=pl.ANY)] * 2,
        out_specs=pl.BlockSpec(memory_space=pl.ANY),
        scratch_shapes=[
            pltpu.VMEM((2, 2, rows, 2 * depth), jnp.bfloat16),
            pltpu.VMEM((2 * depth, half), jnp.bfloat16),
            pltpu.VMEM((chunks, 2 * depth, 2 * LANES), jnp.bfloat16),
            pltpu.VMEM((2, 2, rows, half), jnp.bfloat16),
            pltpu.VMEM((chunks, 2, 2, rows, 2 * LANES), jnp.bfloat16),
            dma, dma, dma, dma, dma((2, 2)), dma((2, 2, 2)),
            dma, dma, dma, dma((chunks,)), dma((2, chunks, 2)), dma((2, chunks)), dma((2, chunks)),
            dma((2, 2)), dma((2, chunks, 2, 2)), dma((4, 2, chunks)),
        ],
        compiler_params=pltpu.CompilerParams(
            collective_id=0, has_side_effects=True, vmem_limit_bytes=60 * 2**20),
    )(tokens, weights)
    row_index = lax.axis_index("gy") * rows + jnp.arange(rows, dtype=jnp.int32)
    return jnp.where((row_index < counts[0] * BLOCK)[:, None], product, jnp.bfloat16(0.0))


def shards(sizes, tokens, weights, counts):
    rows, depth = tokens.shape
    cols = weights.shape[1]
    held = 2 * (12 * rows * cols // 2 + 8 * rows * depth + 6 * depth * cols // 2)
    fits = rows % 16 == 0 and cols % (2 * LANES) == 0 and depth % 128 == 0 and held < 56 * 2**20
    if sizes["groups"] == sizes["gy"] == sizes["gz"] == 2 and sizes["gx"] == 4 and fits:
        return shards_kernel(tokens, weights, counts)
    return shards_general(tokens, weights, counts)


def solution(mesh):
    return jax.shard_map(
        functools.partial(shards, dict(mesh.shape)),
        mesh=mesh,
        in_specs=(P(("groups", "gx", "gz"), "gy"), P("gy", ("gz", "gx")), P(("groups", "gx"))),
        out_specs=P(("groups", "gx", "gy"), "gz"),
        check_vma=False,
    )
```

```python
import functools

import jax
import jax.numpy as jnp
from jax import lax
from jax.experimental import pallas as pl
from jax.experimental.pallas import tpu as pltpu
from jax.sharding import PartitionSpec as P

BLOCK = 128
LANES = 128
MESH = pl.DeviceIdType.MESH


def block_product(left_rows, column_piece, valid_count):
    total_rows = left_rows.shape[0]
    row_index = jnp.arange(total_rows, dtype=jnp.int32)
    product = jnp.dot(left_rows, column_piece, preferred_element_type=jnp.float32)
    return jnp.where((row_index < valid_count * BLOCK)[:, None], product, jnp.float32(0.0))


def shards_general(tokens, weights, counts):
    valid_count = counts[0]
    shard_rows = lax.all_gather(tokens, "gz", axis=0, tiled=True)
    partial_value = block_product(
        shard_rows, lax.all_gather(weights, "gx", axis=1, tiled=True), valid_count
    )
    result = lax.psum_scatter(partial_value, "gy", scatter_dimension=0, tiled=True)
    return result.astype(jnp.bfloat16)


def kernel(tokens, weights, out, t, wo, wr, oo, op,
           load_sem, tx_send, tz_send, td_send, chip_send, t_recv,
           wo_load, wo_send, wo_recv, wr_send, wr_recv, y_send, y_recv,
           oo_send, op_send, o_recv):
    y, z = lax.axis_index("groups"), lax.axis_index("gx")
    g, x = lax.axis_index("gy"), lax.axis_index("gz")
    rows, depth = tokens.shape
    half = weights.shape[1] // 2
    chunks = half // LANES
    side = z // 2
    role = (z + side) % 2
    mate = 4 * side + 1 - z
    far = 2 - side
    hub = role == 1
    line = g == y

    barrier = pltpu.get_barrier_semaphore()
    for d in range(4):
        for e in range(2):
            if d or e:
                pl.semaphore_signal(barrier, inc=1, device_id={"gx": (z + d) % 4, "gy": (g + e) % 2},
                                    device_id_type=MESH)
    pl.semaphore_signal(barrier, inc=1, device_id={"gz": 1 - x}, device_id_type=MESH)
    pl.semaphore_signal(barrier, inc=1, device_id={"groups": 1 - y}, device_id_type=MESH)
    pl.semaphore_wait(barrier, 9)

    def remote(src, dst, send, recv, **where):
        return pltpu.make_async_remote_copy(src, dst, send, recv, device_id=where, device_id_type=MESH)

    def cut(k):
        return pl.ds(pl.multiple_of(k * depth, depth), depth)

    def slot(r, h, k):
        return t.at[r, h, :, cut(k)]

    own = slot(role, x, g)
    load = pltpu.make_async_copy(tokens, own, load_sem)
    to_x = remote(tokens, own, tx_send, t_recv.at[role, x, g], gz=1 - x)
    to_z = remote(tokens, own, tz_send, t_recv.at[role, x, g], gx=mate)
    relay_x = remote(slot(1 - role, x, g), slot(1 - role, x, g), td_send,
                     t_recv.at[1 - role, x, g], gz=1 - x)

    def to_chip(r, h, k):
        src = tokens if r is role and h is x else slot(r, h, k)
        return remote(src, slot(r, h, k), chip_send.at[r, h], t_recv.at[r, h, k], gy=1 - g)

    def arrived(r, h, k):
        return remote(slot(r, h, k), slot(r, h, k), td_send, t_recv.at[r, h, k], gy=1 - g)

    def part(p):
        return pl.ds(pl.multiple_of(p * half, LANES), half)

    wo_mine = pltpu.make_async_copy(weights.at[:, part(g)], wo.at[cut(g)], wo_load)
    wo_other = remote(weights.at[:, part(1 - g)], wo.at[cut(g)], wo_send, wo_recv, gy=1 - g)

    def lanes(ab):
        return pl.ds(pl.multiple_of(ab * LANES, LANES), LANES)

    def push(i):
        src = weights.at[:, pl.ds(pl.multiple_of(y * half + i * LANES, LANES), LANES)]
        return remote(src, wr.at[i, cut(g), lanes(1 - role)], wr_send.at[i],
                      wr_recv.at[1 - role, i, g], gx=far, gy=y)

    def pushed(ab, i, k):
        dst = wr.at[i, cut(k), lanes(ab)]
        return remote(dst, dst, wr_send.at[i], wr_recv.at[ab, i, k], gy=1 - g)

    def pass_on(ab, i):
        dst = wr.at[i, :, lanes(ab)]
        return remote(dst, dst, y_send.at[ab, i], y_recv.at[ab, i], groups=1 - y)

    def layer(r):
        return (1 - r) * 3 * side + r * (1 + side)

    def own_dst(c, p):
        return out.at[:, pl.ds(pl.multiple_of(c * 2 * half + p * half, LANES), half)]

    def far_layer(ab):
        return (1 - ab) * far + ab * 3 * (1 - side)

    def far_dst(ab, p, i):
        return out.at[:, pl.ds(
            pl.multiple_of(far_layer(ab) * 2 * half + p * half + i * LANES, LANES), LANES)]

    def send_own(r, h):
        return remote(oo.at[r, h], own_dst(z, g), oo_send.at[r, h], o_recv.at[role, g, 0],
                      gx=layer(r), gy=h)

    def keep_own():
        return pltpu.make_async_copy(oo.at[role, g], own_dst(z, g), oo_send.at[role, g])

    def send_far(ab, i, r, h):
        return remote(op.at[i, r, h, :, lanes(ab)], far_dst(ab, g, i), op_send.at[ab, i, r, h],
                      o_recv.at[2 + ab, g, i], gx=layer(r), gy=h)

    def keep_far(ab, i):
        return pltpu.make_async_copy(op.at[i, role, g, :, lanes(ab)], far_dst(ab, g, i),
                                     op_send.at[ab, i, role, g])

    to_x.start()
    to_z.start()
    load.start()
    to_chip(role, x, g).start()

    @pl.loop(0, chunks)
    def _(i):
        push(i).start()
    wo_other.start()
    wo_mine.start()

    def pass_step(ab, i):
        @pl.when(hub & line)
        def _():
            pushed(ab, i, 0).wait_recv()
            pushed(ab, i, 1).wait_recv()
            pass_on(ab, i).start()

    def own_half(r):
        @pl.loop(0, 2)
        def _(h):
            @pl.loop(0, half // 256)
            def _(q):
                at = pl.ds(pl.multiple_of(q * 256, 256), 256)
                oo[r, h, :, at] = jnp.dot(
                    t[r, h], wo[:, at], preferred_element_type=jnp.float32).astype(oo.dtype)
            if half % 256:
                at = pl.ds(half // 256 * 256, half % 256)
                oo[r, h, :, at] = jnp.dot(
                    t[r, h], wo[:, at], preferred_element_type=jnp.float32).astype(oo.dtype)
            mine = (r == role) & (h == g)

            @pl.when(mine)
            def _():
                keep_own().start()

            @pl.when(jnp.logical_not(mine))
            def _():
                send_own(r, h).start()

    def far_one(ab, i):
        @pl.when(hub)
        def _():
            @pl.when(jnp.logical_not(line))
            def _():
                pass_on(ab, i).wait_recv()

            at = pl.ds(ab * LANES, LANES)

            @pl.loop(0, 4)
            def _(b):
                r, h = b // 2, b % 2
                op[i, r, h, :, at] = jnp.dot(
                    t[r, h], wr[i, :, at], preferred_element_type=jnp.float32).astype(op.dtype)
                mine = (r == role) & (h == g)

                @pl.when(mine)
                def _():
                    keep_far(ab, i).start()

                @pl.when(jnp.logical_not(mine))
                def _():
                    send_far(ab, i, r, h).start()

    lead = max(1, chunks - 1)
    order = [(0, i) for i in range(lead)]
    for i in range(chunks):
        order.append((1, i))
        if i + lead < chunks:
            order.append((0, i + lead))
    ready = order[::-1]
    order = order[::-1]

    def next_pass():
        if order:
            pass_step(*order.pop())

    next_pass()
    next_pass()
    arrived(role, 1 - x, g).wait_recv()
    to_chip(role, 1 - x, g).start()
    arrived(1 - role, x, g).wait_recv()
    relay_x.start()
    to_chip(1 - role, x, g).start()
    next_pass()
    load.wait()
    arrived(role, x, 1 - g).wait_recv()
    arrived(role, 1 - x, 1 - g).wait_recv()
    wo_mine.wait()
    wo_other.wait()
    next_pass()
    own_half(role)
    next_pass()
    arrived(1 - role, 1 - x, g).wait_recv()
    to_chip(1 - role, 1 - x, g).start()
    next_pass()
    arrived(1 - role, x, 1 - g).wait_recv()
    arrived(1 - role, 1 - x, 1 - g).wait_recv()
    own_half(1 - role)
    while ready:
        next_pass()
        for _ in range(2):
            if len(ready) > len(order):
                far_one(*ready.pop())

    to_x.wait_send()
    to_z.wait_send()
    relay_x.wait_send()
    for b in range(4):
        to_chip(b // 2, b % 2, g).wait_send()

    @pl.loop(0, 4)
    def _(b):
        r, h = b // 2, b % 2
        mine = (r == role) & (h == g)

        @pl.when(mine)
        def _():
            keep_own().wait()

        @pl.when(jnp.logical_not(mine))
        def _():
            send_own(r, h).wait_send()

        @pl.when(jnp.logical_not(mine))
        def _():
            remote(oo.at[0, 0], own_dst(layer(r), h), oo_send.at[0, 0], o_recv.at[r, h, 0],
                   gy=1 - g).wait_recv()

    @pl.loop(0, chunks)
    def _(i):
        push(i).wait_send()

        @pl.loop(0, 2)
        def _(ab):
            @pl.when(hub & line)
            def _():
                pass_on(ab, i).wait_send()

            @pl.when(hub)
            def _():
                keep_far(ab, i).wait()

                @pl.loop(0, 4)
                def _(b):
                    r, h = b // 2, b % 2

                    @pl.when(jnp.logical_not((r == role) & (h == g)))
                    def _():
                        send_far(ab, i, r, h).wait_send()

            @pl.loop(0, 2)
            def _(p):
                @pl.when(jnp.logical_not(hub & (p == g)))
                def _():
                    remote(op.at[0, 0, 0, :, lanes(0)], far_dst(ab, p, i), op_send.at[0, 0, 0, 0],
                           o_recv.at[2 + ab, p, i], gy=1 - g).wait_recv()


def shards_kernel(tokens, weights, counts):
    rows, depth = tokens.shape
    cols = weights.shape[1]
    half = cols // 2
    chunks = half // LANES
    dma = pltpu.SemaphoreType.DMA
    product = pl.pallas_call(
        kernel,
        out_shape=jax.ShapeDtypeStruct((rows, 4 * cols), jnp.bfloat16),
        in_specs=[pl.BlockSpec(memory_space=pl.ANY)] * 2,
        out_specs=pl.BlockSpec(memory_space=pl.ANY),
        scratch_shapes=[
            pltpu.VMEM((2, 2, rows, 2 * depth), jnp.bfloat16),
            pltpu.VMEM((2 * depth, half), jnp.bfloat16),
            pltpu.VMEM((chunks, 2 * depth, 2 * LANES), jnp.bfloat16),
            pltpu.VMEM((2, 2, rows, half), jnp.bfloat16),
            pltpu.VMEM((chunks, 2, 2, rows, 2 * LANES), jnp.bfloat16),
            dma, dma, dma, dma, dma((2, 2)), dma((2, 2, 2)),
            dma, dma, dma, dma((chunks,)), dma((2, chunks, 2)), dma((2, chunks)), dma((2, chunks)),
            dma((2, 2)), dma((2, chunks, 2, 2)), dma((4, 2, chunks)),
        ],
        compiler_params=pltpu.CompilerParams(
            collective_id=0, has_side_effects=True, vmem_limit_bytes=60 * 2**20),
    )(tokens, weights)
    row_index = lax.axis_index("gy") * rows + jnp.arange(rows, dtype=jnp.int32)
    return jnp.where((row_index < counts[0] * BLOCK)[:, None], product, jnp.bfloat16(0.0))


def shards(sizes, tokens, weights, counts):
    rows, depth = tokens.shape
    cols = weights.shape[1]
    held = 2 * (12 * rows * cols // 2 + 8 * rows * depth + 6 * depth * cols // 2)
    fits = rows % 16 == 0 and cols % (2 * LANES) == 0 and depth % 128 == 0 and held < 56 * 2**20
    if sizes["groups"] == sizes["gy"] == sizes["gz"] == 2 and sizes["gx"] == 4 and fits:
        return shards_kernel(tokens, weights, counts)
    return shards_general(tokens, weights, counts)


def solution(mesh):
    return jax.shard_map(
        functools.partial(shards, dict(mesh.shape)),
        mesh=mesh,
        in_specs=(P(("groups", "gx", "gz"), "gy"), P("gy", ("gz", "gx")), P(("groups", "gx"))),
        out_specs=P(("groups", "gx", "gy"), "gz"),
        check_vma=False,
    )
```
